32 devices in a mesh: dp: 8 (over z, x), head: 4 (over y, core).
Axes of the slice: x: 2, y: 2, z: 4, core: 2. Of those that a mesh axis runs over, the one named last changes fastest.
Arguments:
- hidden_in: bfloat16 [8192, 2048], P(('dp', 'head')), may hold values from -6 to 6
- in_gain: float32 [2048], replicated, may hold values from 0.1 to 1.9
- gate_proj: bfloat16 [2048, 4096], P(None, 'head'), may hold values from -0.125 to 0.125
- value_proj: bfloat16 [2048, 4096], P(None, 'head'), may hold values from -0.125 to 0.125
- state_proj: bfloat16 [2048, 256], replicated, may hold values from -0.125 to 0.125
- step_proj: bfloat16 [2048, 64], P(None, 'head'), may hold values from -0.03125 to 0.03125
- conv_value: float32 [4, 4096], P(None, 'head'), may hold values from -3 to 3
- conv_value_bias: float32 [4096], P('head'), may hold values from -3 to 3
- conv_state: float32 [4, 256], replicated, may hold values from -3 to 3
- conv_state_bias: float32 [256], replicated, may hold values from -3 to 3
- step_bias: float32 [64], P('head'), may hold values from -6 to -1
- decay_log: float32 [64], P('head'), may hold values from 0 to 2.77
- skip_gain: float32 [64], P('head'), may hold values from 0.5 to 1.5
- out_gain: float32 [4096], P('head'), may hold values from 0.1 to 1.9
- out_proj: bfloat16 [4096, 2048], P('head'), may hold values from -0.125 to 0.125
- cotangent: bfloat16 [8192, 2048], P(('dp', 'head')), may hold values from -6 to 6
- width_level: int32 [8], P('dp'), may hold values from 0 to 3
Outputs:
- block_out: bfloat16 [8192, 2048], P(('dp', 'head'))
- in_grad: float32 [8192, 2048], P(('dp', 'head'))
- in_gain_grad: float32 [2048], replicated
- gate_proj_grad: float32 [2048, 4096], P('dp', 'head')
- value_proj_grad: float32 [2048, 4096], P('dp', 'head')
- state_proj_grad: float32 [2048, 256], P('dp')
- step_proj_grad: float32 [2048, 64], P('dp', 'head')
- conv_value_grad: float32 [4, 4096], P(None, 'head')
- conv_value_bias_grad: float32 [4096], P('head')
- conv_state_grad: float32 [4, 256], replicated
- conv_state_bias_grad: float32 [256], replicated
- step_bias_grad: float32 [64], P('head')
- decay_log_grad: float32 [64], P('head')
- skip_gain_grad: float32 [64], P('head')
- out_gain_grad: float32 [4096], P('head')
- out_proj_grad: float32 [4096, 2048], P('head', 'dp')
The draws below stay inside these ranges and needn't reach their ends.
All inputs are finite; a program needn't handle non-finite values.
Results may differ from the reference program's by a relative error of at most 0.0079.
Values may be sent and summed in bfloat16 or wider, within the bound.
A program may use at most 192 MiB of HBM per device.

```python
import math
import jax
import jax.numpy as jnp
import numpy as np
from jax import lax

D = 2048
H = 64
P_SIZE = 64
N = 128
K = 4
SPAN = 256
SEQ = 1024
DI = 4096
HL = 16
SEQS = 8
TOKENS = 8192
N_HEAD = 4


def plant(values, key, smallest, largest):
    longest = values.shape.index(max(values.shape))
    spots = []
    for shift in (0, 1):
        where = [jax.random.randint(jax.random.fold_in(key, axis), (), 0, length) for axis, length in enumerate(values.shape)]
        where[longest] = (where[longest] + shift) % values.shape[longest]
        spots.append(tuple(where))
    return values.at[spots[0]].set(smallest).at[spots[1]].set(largest)


def steps_of(own_key, dims, split, low, top_value):
    level, own = 1.0, jax.random.fold_in(own_key, 6)
    for dim, shards_of in split:
        steps = jnp.exp(jax.random.uniform(jax.random.fold_in(own, dim), (shards_of,), jnp.float32, low / len(split), top_value / len(split)))
        level = level * jnp.repeat(steps, dims[dim] // shards_of).reshape([-1 if axis == dim else 1 for axis in range(len(dims))])
    return level


def cumulative_ranks(amount, lean):
    weights = [(1 << 20) // math.isqrt(standing ** lean) + 1 for standing in range(1, amount + 1)]
    width = 1 + sum(weights) // (1 << 30)
    return np.cumsum(np.array([max(1, weight // width) for weight in weights]))


def ranked(key, shape, count, slope):
    grid = cumulative_ranks(count, slope)
    ticket = jax.random.randint(jax.random.fold_in(key, 1), shape, 0, int(grid[count - 1]))
    grade = jnp.searchsorted(jnp.asarray(grid, jnp.int32), ticket, side="right")
    return jax.random.permutation(jax.random.fold_in(key, 2), count)[grade].astype(jnp.int32)


def bell_draw(key, dims, scale, reach, shards=(), held_as=jnp.bfloat16):
    gain = steps_of(key, dims, shards, -0.22, 0.18) if shards else 1.0
    entries = jax.random.normal(key, dims, jnp.float32) * scale * gain
    return jnp.minimum(jnp.maximum(entries, -reach), reach).astype(held_as)


def setup_inputs(seed: int = 0) -> dict:
    key_list = jax.random.split(jax.random.key(seed), 18)
    return {
        "hidden_in": bell_draw(key_list[0], (TOKENS, D), 1.0, 6.0, ((0, 32),)),
        "in_gain": jnp.clip(1.0 + 0.18 * jax.random.normal(key_list[1], (D,), jnp.float32), 0.1, 1.9),
        "gate_proj": bell_draw(key_list[2], (D, DI), D ** -0.5, 0.125, ((1, 4),)),
        "value_proj": bell_draw(key_list[3], (D, DI), D ** -0.5, 0.125, ((1, 4),)),
        "state_proj": bell_draw(key_list[4], (D, 2 * N), D ** -0.5, 0.125),
        "step_proj": bell_draw(key_list[5], (D, H), (16 * D) ** -0.5, 0.03125, ((1, 4),)),
        "conv_value": bell_draw(key_list[6], (K, DI), K ** -0.5, 3.0, ((1, 4),), jnp.float32),
        "conv_value_bias": bell_draw(key_list[7], (DI,), 0.3, 3.0, ((0, 4),), jnp.float32),
        "conv_state": bell_draw(key_list[8], (K, 2 * N), K ** -0.5, 3.0, (), jnp.float32),
        "conv_state_bias": bell_draw(key_list[9], (2 * N,), 0.3, 3.0, (), jnp.float32),
        "step_bias": jnp.clip(-6.0 + 5.0 * jax.random.uniform(key_list[10], (H,), jnp.float32) ** steps_of(key_list[10], (H,), ((0, 4),), -0.2, 0.2), -6.0, -1.0),
        "decay_log": jnp.clip(2.77 * jax.random.uniform(key_list[11], (H,), jnp.float32) ** steps_of(key_list[11], (H,), ((0, 4),), -0.2, 0.2), 0.0, 2.77),
        "skip_gain": jnp.clip(0.5 + 1.0 * jax.random.uniform(key_list[12], (H,), jnp.float32) ** steps_of(key_list[12], (H,), ((0, 4),), -0.2, 0.2), 0.5, 1.5),
        "out_gain": jnp.clip(1.0 + 0.18 * jax.random.normal(key_list[13], (DI,), jnp.float32), 0.1, 1.9),
        "out_proj": bell_draw(key_list[14], (DI, D), (DI // 2) ** -0.5, 0.125, ((0, 4),)),
        "cotangent": bell_draw(key_list[15], (TOKENS, D), 1.0, 6.0, ((0, 32),)),
        "width_level": plant(ranked(key_list[16], (SEQS,), 4, 2), jax.random.fold_in(key_list[16], 3), 0, 3).astype(jnp.int32),
    }


HIGH = lax.Precision.HIGHEST
EPS = 1e-05

@jax.custom_vjp
def low(v):
    return lax.optimization_barrier(v.astype(jnp.bfloat16)).astype(jnp.float32)

@jax.custom_vjp
def low_back(v):
    return v

def low_keep(v):
    return (low(v), None)

def low_pass(kept, grad):
    return (grad,)

def back_keep(v):
    return (v, None)

def back_low(kept, grad):
    return (low(grad),)
low.defvjp(low_keep, low_pass)
low_back.defvjp(back_keep, back_low)

def precise(left, right):
    return jnp.dot(left, right, precision=HIGH)

def conv_causal(series, kernel, shift):
    kernel_len = kernel.shape[0]
    length = series.shape[0]
    padded = jnp.pad(series, ((kernel_len - 1, 0), (0, 0)))
    running = shift[None, :] + kernel[0][None, :] * padded[0:length]
    for offset in range(1, kernel_len):
        running = running + kernel[offset][None, :] * padded[offset:offset + length]
    return running

def state_space(inputs, step_size, decay_rate, key_rows, query_rows, skip_gain):
    seq_len, heads, head_dim = inputs.shape
    blocks = seq_len // SPAN
    values = inputs.reshape(blocks, SPAN, heads, head_dim)
    deltas = step_size.reshape(blocks, SPAN, heads)
    keys = key_rows.reshape(blocks, SPAN, -1)
    queries = query_rows.reshape(blocks, SPAN, -1)
    cumul = jnp.cumsum(deltas * decay_rate[None, None, :], axis=1)
    inner = jnp.einsum('cin,cjn->cij', queries, keys, precision=HIGH)
    lower = (jnp.arange(SPAN)[:, None] >= jnp.arange(SPAN)[None, :])[None, :, :, None]
    spread = cumul[:, :, None, :] - cumul[:, None, :, :]
    mixing = jnp.where(lower, jnp.exp(jnp.where(lower, spread, 0.0)), 0.0) * inner[:, :, :, None]
    scaled = values * deltas[:, :, :, None]
    within = jnp.einsum('cijh,cjhp->cihp', mixing, scaled, precision=HIGH)
    tails = jnp.exp(cumul[:, -1:, :] - cumul)
    states = jnp.einsum('cjhp,cjn->chpn', scaled * tails[:, :, :, None], keys, precision=HIGH)
    totals = jnp.exp(cumul[:, -1, :])

    def carry_state(state, item):
        fresh, factor = item
        return (factor[:, None, None] * state + fresh, state)
    start = jnp.zeros((heads, head_dim, keys.shape[2]), dtype=inputs.dtype)
    _, entering = lax.scan(carry_state, start, (states, totals))
    across = jnp.einsum('cin,chpn->cihp', queries, entering, precision=HIGH) * jnp.exp(cumul)[:, :, :, None]
    result = within + across + values * skip_gain[None, None, :, None]
    return result.reshape(seq_len, heads, head_dim)

def mix_block(value_pre, state_pre, step_pre, gate_pre, conv_value, conv_value_bias, conv_state, conv_state_bias, step_bias, decay_log, skip_gain, keep):
    seq_len = value_pre.shape[0]
    heads = step_pre.shape[1]
    value_act = jax.nn.silu(conv_causal(value_pre, conv_value, conv_value_bias))
    state_act = jax.nn.silu(conv_causal(state_pre, conv_state, conv_state_bias))
    half = state_act.shape[1] // 2
    step_size = jax.nn.softplus(step_pre + step_bias[None, :])
    inputs = value_act.reshape(seq_len, heads, -1) * keep[None, :, None]
    result = state_space(inputs, step_size, -jnp.exp(decay_log), state_act[:, :half], state_act[:, half:], skip_gain)
    return result.reshape(seq_len, -1) * jax.nn.silu(gate_pre)

def residual_layer(resid, weights, keep, token_count):
    in_gain, gate_proj, value_proj, state_proj, step_proj, conv_value, conv_value_bias, conv_state, conv_state_bias, step_bias, decay_log, skip_gain, out_gain, out_proj = weights
    normed = low(resid * lax.rsqrt(lax.optimization_barrier(jnp.mean(resid * resid, axis=-1, keepdims=True)) + EPS) * in_gain)
    gate_pre = low_back(precise(normed, gate_proj))
    value_pre = low_back(precise(normed, value_proj))
    state_pre = low_back(precise(normed, state_proj))
    step_pre = low_back(precise(normed, step_proj))
    gated = mix_block(value_pre, state_pre, step_pre, gate_pre, conv_value, conv_value_bias, conv_state, conv_state_bias, step_bias, decay_log, skip_gain, keep)
    squares = lax.optimization_barrier(jnp.sum(gated * gated, axis=-1, keepdims=True))
    normed_out = low(gated * lax.rsqrt(squares / token_count + EPS) * out_gain)
    return resid + precise(normed_out, out_proj)

def reference(hidden_in, in_gain, gate_proj, value_proj, state_proj, step_proj, conv_value, conv_value_bias, conv_state, conv_state_bias, step_bias, decay_log, skip_gain, out_gain, out_proj, cotangent, width_level):
    weights = tuple((w.astype(jnp.float32) for w in (in_gain, gate_proj, value_proj, state_proj, step_proj, conv_value, conv_value_bias, conv_state, conv_state_bias, step_bias, decay_log, skip_gain, out_gain, out_proj)))
    rows_all = hidden_in.astype(jnp.float32).reshape(-1, SEQ, D)
    grads_all = cotangent.astype(jnp.float32).reshape(-1, SEQ, D)
    head_ids = jnp.arange(H)

    def per_sequence(carry, item):
        resid, grad_out, level = item
        active = jnp.right_shift(HL, 3 - level)
        keep = (head_ids % HL < active).astype(resid.dtype)
        token_count = (active * N_HEAD * P_SIZE).astype(resid.dtype)

        def apply_layer(resid_in, *params):
            return residual_layer(resid_in, params, keep, token_count)
        result, pull = jax.vjp(apply_layer, resid, *weights)
        grads = pull(grad_out)
        summed = tuple((c + g for c, g in zip(carry, grads[1:])))
        return (summed, (result, grads[0]))
    start = tuple((jnp.zeros_like(w) for w in weights))
    sums, (results, in_grads) = lax.scan(per_sequence, start, (rows_all, grads_all, width_level))
    return (results.reshape(TOKENS, D).astype(jnp.bfloat16), in_grads.reshape(TOKENS, D), sums[0], sums[1], sums[2], sums[3], sums[4], sums[5], sums[6], sums[7], sums[8], sums[9], sums[10], sums[11], sums[12], sums[13])
```

```python
import functools
import jax
import jax.numpy as jnp
from jax import lax
from jax.experimental import pallas as pl
from jax.experimental.pallas import tpu as pltpu
from jax.sharding import PartitionSpec as P

F32 = jnp.float32
BF = jnp.bfloat16
LANES = 128
EPS = 1e-05


def mm(a, b):
    return jnp.dot(a, b, preferred_element_type=F32)


def mm_t(a, b):
    return lax.dot_general(a, b, (((1,), (1,)), ((), ())), preferred_element_type=F32)


def t_mm(a, b):
    return lax.dot_general(a, b, (((0,), (0,)), ((), ())), preferred_element_type=F32)


def sigmoid(v):
    return 0.5 * jnp.tanh(0.5 * v) + 0.5


def softplus(v):
    return jnp.maximum(v, 0.0) + jnp.log1p(jnp.exp(-jnp.abs(v)))


def split3(v):
    hi = v.astype(BF)
    rest = v - hi.astype(F32)
    mid = rest.astype(BF)
    low = (rest - mid.astype(F32)).astype(BF)
    return hi, mid, low


def split2(v):
    hi = v.astype(BF)
    return hi, (v - hi.astype(F32)).astype(BF)


def exact_left(ones, v):
    hi, mid, low = split3(v)
    return mm(ones, hi) + mm(ones, mid) + mm(ones, low)


def conv(buf, first, taps, length):
    out = taps[0][None] * buf[pl.ds(first, length), :]
    for k in range(1, len(taps)):
        out = out + taps[k][None] * buf[pl.ds(first + k, length), :]
    return out


def scan_parts(step_pre, bias, rate, span):
    raw = step_pre + bias
    size = softplus(raw)
    row = lax.broadcasted_iota(jnp.int32, (span, span), 0)
    col = lax.broadcasted_iota(jnp.int32, (span, span), 1)
    tri = (row >= col).astype(BF)
    cum = exact_left(tri, size * rate)
    return raw, size, cum, row, col


def spread_heads(values, expand):
    hi, low = split2(values)
    return mm(hi, expand) + mm(low, expand)


def fwd_kernel(
    span, heads, taps_n, vp_ref, ss_ref, cv_ref, cs_ref, hv_ref, ex_ref,
    ssd_ref, ent_ref, state, vbuf, sbuf,
):
    chans = vp_ref.shape[1]
    maps = cs_ref.shape[1]
    nst = maps // 2
    halo = taps_n - 1

    @pl.when(pl.program_id(0) == 0)
    def _():
        state[...] = jnp.zeros_like(state)
        vbuf[0:8, :] = jnp.zeros((8, chans), F32)
        sbuf[0:8, :] = jnp.zeros((8, maps), F32)

    vbuf[8 : 8 + span, :] = vp_ref[...].astype(F32)
    sbuf[8 : 8 + span, :] = ss_ref[:, :maps]
    taps = [cv_ref[k] for k in range(taps_n)]
    pre = conv(vbuf, 8 - halo, taps, span) + cv_ref[4][None]
    staps = [cs_ref[k] for k in range(taps_n)]
    spre = conv(sbuf, 8 - halo, staps, span) + cs_ref[4][None]
    vbuf[0:8, :] = vbuf[span : span + 8, :]
    sbuf[0:8, :] = sbuf[span : span + 8, :]
    sact = spre * sigmoid(spre)
    key = sact[:, :nst].astype(BF)
    query = sact[:, nst:].astype(BF)
    x = pre * sigmoid(pre) * cv_ref[6][None]
    _, size, cum, row, col = scan_parts(ss_ref[:, maps:], hv_ref[0][None], hv_ref[1][None], span)
    expand = ex_ref[...]
    last = cum[span - 1 : span, :]
    size_e = spread_heads(size, expand)
    ecum_e = spread_heads(jnp.exp(cum), expand)
    tail_e = spread_heads(jnp.exp(last - cum), expand)
    etot_e = spread_heads(jnp.broadcast_to(jnp.exp(last), (8, LANES)), expand)[0:1]
    xs = x * size_e
    xs_low = xs.astype(BF)
    before = state[...]
    before_low = before.astype(BF)
    ent_ref[0] = before_low
    inter = mm(query, before_low) * ecum_e
    state[...] = before * etot_e + t_mm(key, (xs * tail_e).astype(BF))
    inner = mm_t(query, key)
    cum_t = jnp.transpose(cum)
    keepm = row >= col
    left = lax.broadcasted_iota(jnp.int32, (span, LANES), 1) < LANES // 2
    for pair in range(heads // 2):
        lanes = slice(pair * LANES, (pair + 1) * LANES)
        part = []
        for h in (2 * pair, 2 * pair + 1):
            diff = cum[:, h : h + 1] - cum_t[h : h + 1, :]
            mix = jnp.exp(jnp.where(keepm, diff, -1e30)) * inner
            part.append(mm(mix.astype(BF), xs_low[:, lanes]))
        within = jnp.where(left, part[0], part[1])
        ssd_ref[:, lanes] = (within + inter[:, lanes] + x[:, lanes] * cv_ref[5:6, lanes]).astype(ssd_ref.dtype)


def bwd_kernel(
    span, heads, taps_n, vp_ref, vh_ref, ss_ref, sh_ref, dy_ref, ent_ref, cv_ref, cs_ref, hv_ref, ex_ref,
    dv_ref, ds_ref, gcv_ref, gcs_ref, gh_ref, dstate, vbuf, sbuf, dvbuf, dsbuf,
):
    chans = vp_ref.shape[1]
    maps = cs_ref.shape[1]
    nst = maps // 2
    halo = taps_n - 1
    step = pl.program_id(0)
    first = step == 0
    start = step == pl.num_programs(0) - 1

    @pl.when(first)
    def _():
        dstate[...] = jnp.zeros_like(dstate)
        dvbuf[span : span + 8, :] = jnp.zeros((8, chans), F32)
        dsbuf[span : span + 8, :] = jnp.zeros((8, maps), F32)
        gcv_ref[...] = jnp.zeros_like(gcv_ref)
        gcs_ref[...] = jnp.zeros_like(gcs_ref)
        gh_ref[...] = jnp.zeros_like(gh_ref)

    vbuf[0:8, :] = jnp.where(start, 0.0, vh_ref[...].astype(F32))
    sbuf[0:8, :] = jnp.where(start, 0.0, sh_ref[:, :maps])
    vbuf[8 : 8 + span, :] = vp_ref[...].astype(F32)
    sbuf[8 : 8 + span, :] = ss_ref[:, :maps]
    taps = [cv_ref[k] for k in range(taps_n)]
    pre = conv(vbuf, 8 - halo, taps, span) + cv_ref[4][None]
    staps = [cs_ref[k] for k in range(taps_n)]
    spre = conv(sbuf, 8 - halo, staps, span) + cs_ref[4][None]
    ssig = sigmoid(spre)
    sact = spre * ssig
    key = sact[:, :nst].astype(BF)
    query = sact[:, nst:].astype(BF)
    sig = sigmoid(pre)
    keep = cv_ref[6][None]
    x = pre * sig * keep
    rate = hv_ref[1][None]
    raw, size, cum, row, col = scan_parts(ss_ref[:, maps:], hv_ref[0][None], rate, span)
    expand = ex_ref[...]
    last = cum[span - 1 : span, :]
    size_e = spread_heads(size, expand)
    ecum_e = spread_heads(jnp.exp(cum), expand)
    tail_e = spread_heads(jnp.exp(last - cum), expand)
    etot_e = spread_heads(jnp.broadcast_to(jnp.exp(last), (8, LANES)), expand)[0:1]
    xs = x * size_e
    xs_low = xs.astype(BF)
    xt = xs * tail_e
    xt_low = xt.astype(BF)
    dy_low = dy_ref[...].astype(BF)
    dy = dy_low.astype(F32)
    before_low = ent_ref[0]
    dz = dy * ecum_e
    dz_low = dz.astype(BF)
    d_after = dstate[...]
    d_after_low = d_after.astype(BF)
    inter = mm(query, before_low)
    w = mm(key, d_after_low)
    d_query = mm_t(dz_low, before_low)
    d_key = mm_t(xt_low, d_after_low)
    through = jnp.sum(d_after * before_low.astype(F32), axis=0, keepdims=True) * etot_e
    dstate[...] = d_after * etot_e + t_mm(query, dz_low)
    inner_t = mm_t(key, query)
    cum_t = jnp.transpose(cum)
    keepm = row <= col
    lane = lax.broadcasted_iota(jnp.int32, (span, LANES), 1)
    left = lane < LANES // 2
    d_inner_t = jnp.zeros((span, span), F32)
    cols = jnp.zeros((span, LANES), F32)
    rows = []
    dxs_parts = []
    zero = jnp.zeros((span, LANES), BF)
    for pair in range(heads // 2):
        lanes = slice(pair * LANES, (pair + 1) * LANES)
        part = []
        xp = xs_low[:, lanes]
        dyp = dy_low[:, lanes]
        for h, mine in ((2 * pair, left), (2 * pair + 1, jnp.logical_not(left))):
            diff = cum_t[h : h + 1, :] - cum[:, h : h + 1]
            decay = jnp.exp(jnp.where(keepm, diff, -1e30))
            mix = decay * inner_t
            part.append(mm(mix.astype(BF), dyp))
            d_mix = mm_t(jnp.where(mine, xp, zero), dyp) * decay
            d_inner_t = d_inner_t + d_mix
            seg = d_mix * inner_t
            rows.append(jnp.sum(seg, axis=0, keepdims=True))
            cols = cols + jnp.where(lane == h, jnp.sum(seg, axis=1, keepdims=True), 0.0)
        dxs_parts.append(jnp.where(left, part[0], part[1]))
    rows.append(jnp.zeros((LANES - heads, span), F32))
    row_sums = jnp.transpose(jnp.concatenate(rows, axis=0))
    dxs = jnp.concatenate(dxs_parts, axis=1) + w * tail_e
    d_inner_low = d_inner_t.astype(BF)
    d_key = d_key + mm(d_inner_low, query)
    d_query = d_query + t_mm(d_inner_low, key)

    gather = functools.partial(mm_t, b=expand)
    r_inter = gather((dz * inter).astype(BF))
    c_tail = gather((xt * w).astype(BF))
    d_size = gather((dxs * x).astype(BF))
    d_skip = gather((dy * x).astype(BF))
    d_tot = gather(jnp.broadcast_to(through, (8, chans)).astype(BF))[0:1]
    later = (row <= col).astype(BF)
    earlier = (row > col).astype(BF)
    d_la = exact_left(later, row_sums - cols + r_inter) + exact_left(earlier, c_tail) + d_tot
    d_step = (d_size + rate * d_la) * sigmoid(raw)
    gh_ref[0:1, :] = gh_ref[0:1, :] + jnp.sum(d_step, axis=0, keepdims=True)
    gh_ref[1:2, :] = gh_ref[1:2, :] + jnp.sum(d_la * size, axis=0, keepdims=True) * rate
    gh_ref[2:3, :] = gh_ref[2:3, :] + jnp.sum(d_skip, axis=0, keepdims=True)

    d_pre = (dxs * size_e + dy * cv_ref[5][None]) * keep * (sig * (1.0 + pre * (1.0 - sig)))
    dvbuf[0:span, :] = d_pre
    dv = taps[taps_n - 1][None] * d_pre
    for k in range(taps_n - 1):
        dv = dv + taps[k][None] * dvbuf[pl.ds(halo - k, span), :]
    dv_ref[...] = dv.astype(dv_ref.dtype)
    for k in range(taps_n):
        gcv_ref[k : k + 1, :] = gcv_ref[k : k + 1, :] + jnp.sum(
            d_pre * vbuf[pl.ds(8 - halo + k, span), :], axis=0, keepdims=True
        )
    gcv_ref[4:5, :] = gcv_ref[4:5, :] + jnp.sum(d_pre, axis=0, keepdims=True)
    dvbuf[span : span + 8, :] = dvbuf[0:8, :]

    d_spre = jnp.concatenate([d_key, d_query], axis=1) * (ssig * (1.0 + spre * (1.0 - ssig)))
    dsbuf[0:span, :] = d_spre
    dsv = staps[taps_n - 1][None] * d_spre
    for k in range(taps_n - 1):
        dsv = dsv + staps[k][None] * dsbuf[pl.ds(halo - k, span), :]
    ds_ref[:, :maps] = dsv.astype(ds_ref.dtype)
    ds_ref[:, maps:] = d_step.astype(ds_ref.dtype)
    for k in range(taps_n):
        gcs_ref[k : k + 1, :] = gcs_ref[k : k + 1, :] + jnp.sum(
            d_spre * sbuf[pl.ds(8 - halo + k, span), :], axis=0, keepdims=True
        )
    gcs_ref[4:5, :] = gcs_ref[4:5, :] + jnp.sum(d_spre, axis=0, keepdims=True)
    dsbuf[span : span + 8, :] = dsbuf[0:8, :]


def full(shape):
    return pl.BlockSpec(shape, lambda i: (0,) * len(shape))


def scan_fwd(vp, ss, cv, cs, hv, ex, heads, taps_n, span):
    rows, chans = vp.shape
    wide = ss.shape[1]
    maps = cs.shape[1]
    nb = rows // span
    return pl.pallas_call(
        functools.partial(fwd_kernel, span, heads, taps_n),
        grid=(nb,),
        in_specs=[
            pl.BlockSpec((span, chans), lambda i: (i, 0)),
            pl.BlockSpec((span, wide), lambda i: (i, 0)),
            full(cv.shape), full(cs.shape), full(hv.shape), full(ex.shape),
        ],
        out_specs=[
            pl.BlockSpec((span, chans), lambda i: (i, 0)),
            pl.BlockSpec((1, maps // 2, chans), lambda i: (i, 0, 0)),
        ],
        out_shape=[
            jax.ShapeDtypeStruct((rows, chans), F32),
            jax.ShapeDtypeStruct((nb, maps // 2, chans), BF),
        ],
        scratch_shapes=[
            pltpu.VMEM((maps // 2, chans), F32),
            pltpu.VMEM((span + 8, chans), F32),
            pltpu.VMEM((span + 8, maps), F32),
        ],
        compiler_params=pltpu.CompilerParams(
            dimension_semantics=("arbitrary",), vmem_limit_bytes=40 << 20),
        name="scan_fwd",
    )(vp, ss, cv, cs, hv, ex)


def scan_bwd(vp, ss, dy, ent, cv, cs, hv, ex, heads, taps_n, span):
    rows, chans = vp.shape
    wide = ss.shape[1]
    maps = cs.shape[1]
    nb = rows // span
    eights = span // 8
    back = lambda i: (nb - 1 - i, 0)
    halo = lambda i: (jnp.maximum((nb - 1 - i) * eights - 1, 0), 0)
    return pl.pallas_call(
        functools.partial(bwd_kernel, span, heads, taps_n),
        grid=(nb,),
        in_specs=[
            pl.BlockSpec((span, chans), back),
            pl.BlockSpec((8, chans), halo),
            pl.BlockSpec((span, wide), back),
            pl.BlockSpec((8, wide), halo),
            pl.BlockSpec((span, chans), back),
            pl.BlockSpec((1, maps // 2, chans), lambda i: (nb - 1 - i, 0, 0)),
            full(cv.shape), full(cs.shape), full(hv.shape), full(ex.shape),
        ],
        out_specs=[
            pl.BlockSpec((span, chans), back),
            pl.BlockSpec((span, wide), back),
            full((8, chans)), full((8, maps)), full((8, LANES)),
        ],
        out_shape=[
            jax.ShapeDtypeStruct((rows, chans), BF),
            jax.ShapeDtypeStruct((rows, wide), BF),
            jax.ShapeDtypeStruct((8, chans), F32),
            jax.ShapeDtypeStruct((8, maps), F32),
            jax.ShapeDtypeStruct((8, LANES), F32),
        ],
        scratch_shapes=[
            pltpu.VMEM((maps // 2, chans), F32),
            pltpu.VMEM((span + 8, chans), F32),
            pltpu.VMEM((span + 8, maps), F32),
            pltpu.VMEM((span + 8, chans), F32),
            pltpu.VMEM((span + 8, maps), F32),
        ],
        compiler_params=pltpu.CompilerParams(
            dimension_semantics=("arbitrary",), vmem_limit_bytes=48 << 20),
        name="scan_bwd",
    )(vp, vp, ss, ss, dy, ent, cv, cs, hv, ex)


def tables(conv_value, conv_value_bias, conv_state, conv_state_bias, step_bias, decay_log, skip_gain, keep, out_gain):
    heads = step_bias.shape[0]
    chans = conv_value.shape[1]
    head_dim = chans // heads
    row = lambda v: v[None, :]
    wide = lambda v: jnp.repeat(v, head_dim)[None, :]
    cv = jnp.concatenate([conv_value, row(conv_value_bias), wide(skip_gain), wide(keep), row(out_gain)], axis=0)
    cs = jnp.concatenate([conv_state, row(conv_state_bias), jnp.zeros((3, conv_state.shape[1]), F32)], axis=0)
    lanes = lambda v: jnp.pad(v, (0, LANES - heads))[None, :]
    hv = jnp.concatenate([lanes(step_bias), lanes(-jnp.exp(decay_log)), jnp.zeros((6, LANES), F32)], axis=0)
    head_of = lax.broadcasted_iota(jnp.int32, (LANES, chans), 1) // head_dim
    ex = (head_of == lax.broadcasted_iota(jnp.int32, (LANES, chans), 0)).astype(BF)
    return cv, cs, hv, ex


def sums_kernel(ssd_ref, gate_ref, dno_ref, cv_ref, out_ref):
    gate = gate_ref[...].astype(F32)
    gated = ssd_ref[...].astype(F32) * gate * sigmoid(gate)
    squares = jnp.sum(gated * gated, axis=1, keepdims=True)
    stat = jnp.sum(dno_ref[...].astype(F32) * cv_ref[7][None] * gated, axis=1, keepdims=True)
    lane = lax.broadcasted_iota(jnp.int32, (gated.shape[0], LANES), 1)
    both = jnp.where(lane == 0, squares, jnp.where(lane == 1, stat, 0.0))
    out_ref[...] = jnp.transpose(both)[0:8]


def row_sums_of(ssd, gate, dno, cv):
    rows, chans = ssd.shape
    span = 256
    tile = pl.BlockSpec((span, chans), lambda i: (i, 0))
    return pl.pallas_call(
        sums_kernel,
        grid=(rows // span,),
        in_specs=[tile, tile, tile, full(cv.shape)],
        out_specs=pl.BlockSpec((8, span), lambda i: (0, i)),
        out_shape=jax.ShapeDtypeStruct((8, rows), F32),
        compiler_params=pltpu.CompilerParams(
            dimension_semantics=("arbitrary",), vmem_limit_bytes=40 << 20),
        name="row_sums",
    )(ssd, gate, dno, cv)


def norm_kernel(ssd_ref, gate_ref, dno_ref, cv_ref, sums_ref, count_ref, no_ref, dy_ref, dg_ref, og_ref):
    @pl.when(pl.program_id(0) == 0)
    def _():
        og_ref[...] = jnp.zeros_like(og_ref)

    span = ssd_ref.shape[0]
    per = jnp.transpose(jnp.concatenate([sums_ref[...], jnp.zeros((LANES - 8, span), F32)], axis=0))
    count = count_ref[0, 0]
    scale = lax.rsqrt(per[:, 0:1] / count + EPS)
    coef = scale * scale * scale * (per[:, 1:2] / count)
    gate = gate_ref[...].astype(F32)
    ssd = ssd_ref[...].astype(F32)
    sig = sigmoid(gate)
    act = gate * sig
    gated = ssd * act
    gain = cv_ref[7][None]
    dno = dno_ref[...].astype(F32)
    unit = gated * scale
    no_ref[...] = (unit * gain).astype(no_ref.dtype)
    d_gated = dno * gain * scale - gated * coef
    dy_ref[...] = (d_gated * act).astype(dy_ref.dtype)
    dg_ref[...] = (d_gated * ssd * (sig * (1.0 + gate * (1.0 - sig)))).astype(dg_ref.dtype)
    og_ref[0:1, :] = og_ref[0:1, :] + jnp.sum(dno * unit, axis=0, keepdims=True)


def norm_both(ssd, gate, dno, cv, sums, count):
    rows, chans = ssd.shape
    span = 256
    tile = pl.BlockSpec((span, chans), lambda i: (i, 0))
    low = jax.ShapeDtypeStruct((rows, chans), BF)
    return pl.pallas_call(
        norm_kernel,
        grid=(rows // span,),
        in_specs=[
            tile, tile, tile, full(cv.shape),
            pl.BlockSpec((8, span), lambda i: (0, i)),
            pl.BlockSpec(memory_space=pltpu.SMEM),
        ],
        out_specs=[tile, tile, tile, full((8, chans))],
        out_shape=[low, low, low, jax.ShapeDtypeStruct((8, chans), F32)],
        compiler_params=pltpu.CompilerParams(
            dimension_semantics=("arbitrary",), vmem_limit_bytes=40 << 20),
        name="norm_both",
    )(ssd, gate, dno, cv, sums, count)


def per_device(
    hidden_in, in_gain, gate_proj, value_proj, state_proj, step_proj, conv_value, conv_value_bias,
    conv_state, conv_state_bias, step_bias, decay_log, skip_gain, out_gain, out_proj, cotangent, width_level,
):
    heads = step_bias.shape[0]
    chans = conv_value.shape[1]
    head_dim = chans // heads
    maps = conv_state.shape[1]
    taps_n = conv_value.shape[0]
    groups = lax.axis_size("head")
    model = hidden_in.shape[1]
    assert width_level.shape[0] == 1 and 2 * head_dim == LANES and heads <= LANES
    span = 128

    resid = hidden_in.astype(F32)
    in_scale = lax.rsqrt(jnp.mean(resid * resid, axis=-1, keepdims=True) + EPS)
    normed = (resid * in_scale * in_gain).astype(BF)
    whole = lax.all_gather(normed, "head", axis=0, tiled=True)
    cot_all = lax.all_gather(cotangent, "head", axis=0, tiled=True)
    side_proj = jnp.concatenate(
        [state_proj, step_proj, jnp.zeros((model, LANES - heads), BF)], axis=1)

    active = jnp.right_shift(heads, 3 - width_level[0])
    keep = (jnp.arange(heads) < active).astype(F32)
    count = (active * groups * head_dim).astype(F32).reshape(1, 1)
    cv, cs, hv, ex = tables(
        conv_value, conv_value_bias, conv_state, conv_state_bias, step_bias, decay_log, skip_gain, keep, out_gain)

    value_pre = mm(whole, value_proj)
    side_pre = mm(whole, side_proj)
    gate_pre = mm(whole, gate_proj)
    ssd, entering = scan_fwd(value_pre, side_pre, cv, cs, hv, ex, heads, taps_n, span)
    d_normed_out = mm_t(cot_all, out_proj)
    sums = row_sums_of(ssd, gate_pre, d_normed_out, cv)
    sums = jnp.pad(lax.psum(sums[:2], "head"), ((0, 6), (0, 0)))
    normed_out, dy, d_gate, og = norm_both(ssd, gate_pre, d_normed_out, cv, sums, count)
    out_part = mm(normed_out, out_proj).astype(BF)
    own_out = lax.psum_scatter(out_part, "head", scatter_dimension=0, tiled=True)
    out_proj_grad = lax.psum_scatter(
        t_mm(normed_out, cot_all).astype(BF), "dp", scatter_dimension=1, tiled=True).astype(F32)
    gate_proj_grad = lax.psum_scatter(
        t_mm(whole, d_gate).astype(BF), "dp", scatter_dimension=0, tiled=True).astype(F32)
    d_value, d_side, gcv, gcs, gh = scan_bwd(
        value_pre, side_pre, dy, entering, cv, cs, hv, ex, heads, taps_n, span)
    value_proj_grad = lax.psum_scatter(
        t_mm(whole, d_value).astype(BF), "dp", scatter_dimension=0, tiled=True).astype(F32)
    d_normed = (mm_t(d_gate, gate_proj) + mm_t(d_value, value_proj) + mm_t(d_side, side_proj)).astype(BF)
    d_normed = lax.psum_scatter(d_normed, "head", scatter_dimension=0, tiled=True).astype(F32)
    side_grad = lax.psum_scatter(
        t_mm(whole, d_side).astype(BF), "dp", scatter_dimension=0, tiled=True).astype(F32)
    step_proj_grad = side_grad[:, maps : maps + heads]
    block_out = (resid + own_out.astype(F32)).astype(BF)
    scaled = d_normed * in_gain
    in_grad = (
        cotangent.astype(F32) + scaled * in_scale
        - resid * in_scale**3 * jnp.sum(scaled * resid, axis=-1, keepdims=True) / model
    )
    in_gain_part = jnp.sum(d_normed * resid * in_scale, axis=0)
    over_head = lax.psum(
        (jnp.concatenate([gcs.reshape(-1), in_gain_part]), side_grad[:, :maps]), "head")
    state_proj_grad = over_head[1]
    packed = lax.psum(jnp.concatenate([over_head[0], gcv.reshape(-1), gh.reshape(-1), og[0]]), "dp")
    at = 8 * maps
    gcs = packed[:at].reshape(8, maps)
    in_gain_grad = packed[at : at + model]
    at = at + model
    gcv = packed[at : at + 8 * chans].reshape(8, chans)
    at = at + 8 * chans
    gh = packed[at : at + 8 * LANES].reshape(8, LANES)
    og = packed[at + 8 * LANES :]
    return (
        block_out, in_grad, in_gain_grad, gate_proj_grad, value_proj_grad, state_proj_grad, step_proj_grad,
        gcv[:taps_n], gcv[4], gcs[:taps_n], gcs[4], gh[0, :heads], gh[1, :heads], gh[2, :heads], og, out_proj_grad,
    )


def solution(mesh):
    placed = (
        P(("dp", "head"), None),
        P(),
        P(None, "head"),
        P(None, "head"),
        P(),
        P(None, "head"),
        P(None, "head"),
        P("head"),
        P(),
        P(),
        P("head"),
        P("head"),
        P("head"),
        P("head"),
        P("head", None),
        P(("dp", "head"), None),
        P("dp"),
    )
    return jax.shard_map(
        per_device,
        mesh=mesh,
        in_specs=placed,
        out_specs=(
            P(("dp", "head"), None),
            P(("dp", "head"), None),
            P(),
            P("dp", "head"),
            P("dp", "head"),
            P("dp", None),
            P("dp", "head"),
            P(None, "head"),
            P("head"),
            P(),
            P(),
            P("head"),
            P("head"),
            P("head"),
            P("head"),
            P("head", "dp"),
        ),
        check_vma=False,
    )
```

```python
import functools
import jax
import jax.numpy as jnp
from jax import lax
from jax.experimental import pallas as pl
from jax.experimental.pallas import tpu as pltpu
from jax.sharding import PartitionSpec as P

F32 = jnp.float32
BF = jnp.bfloat16
LANES = 128
EPS = 1e-05


def mm(a, b):
    return jnp.dot(a, b, preferred_element_type=F32)


def mm_t(a, b):
    return lax.dot_general(a, b, (((1,), (1,)), ((), ())), preferred_element_type=F32)


def t_mm(a, b):
    return lax.dot_general(a, b, (((0,), (0,)), ((), ())), preferred_element_type=F32)


def sigmoid(v):
    return 0.5 * jnp.tanh(0.5 * v) + 0.5


def softplus(v):
    return jnp.maximum(v, 0.0) + jnp.log1p(jnp.exp(-jnp.abs(v)))


def split3(v):
    hi = v.astype(BF)
    rest = v - hi.astype(F32)
    mid = rest.astype(BF)
    low = (rest - mid.astype(F32)).astype(BF)
    return hi, mid, low


def split2(v):
    hi = v.astype(BF)
    return hi, (v - hi.astype(F32)).astype(BF)


def exact_left(ones, v):
    hi, mid, low = split3(v)
    return mm(ones, hi) + mm(ones, mid) + mm(ones, low)


def conv(buf, first, taps, length):
    out = taps[0][None] * buf[pl.ds(first, length), :]
    for k in range(1, len(taps)):
        out = out + taps[k][None] * buf[pl.ds(first + k, length), :]
    return out


def scan_parts(step_pre, bias, rate, span):
    raw = step_pre + bias
    size = softplus(raw)
    row = lax.broadcasted_iota(jnp.int32, (span, span), 0)
    col = lax.broadcasted_iota(jnp.int32, (span, span), 1)
    tri = (row >= col).astype(BF)
    cum = exact_left(tri, size * rate)
    return raw, size, cum, row, col


def spread_heads(values, expand):
    hi, low = split2(values)
    return mm(hi, expand) + mm(low, expand)


def fwd_kernel(
    span, heads, taps_n, vp_ref, ss_ref, cv_ref, cs_ref, hv_ref, ex_ref,
    ssd_ref, ent_ref, state, vbuf, sbuf,
):
    chans = vp_ref.shape[1]
    maps = cs_ref.shape[1]
    nst = maps // 2
    halo = taps_n - 1

    @pl.when(pl.program_id(0) == 0)
    def _():
        state[...] = jnp.zeros_like(state)
        vbuf[0:8, :] = jnp.zeros((8, chans), F32)
        sbuf[0:8, :] = jnp.zeros((8, maps), F32)

    vbuf[8 : 8 + span, :] = vp_ref[...].astype(F32)
    sbuf[8 : 8 + span, :] = ss_ref[:, :maps]
    taps = [cv_ref[k] for k in range(taps_n)]
    pre = conv(vbuf, 8 - halo, taps, span) + cv_ref[4][None]
    staps = [cs_ref[k] for k in range(taps_n)]
    spre = conv(sbuf, 8 - halo, staps, span) + cs_ref[4][None]
    vbuf[0:8, :] = vbuf[span : span + 8, :]
    sbuf[0:8, :] = sbuf[span : span + 8, :]
    sact = spre * sigmoid(spre)
    key = sact[:, :nst].astype(BF)
    query = sact[:, nst:].astype(BF)
    x = pre * sigmoid(pre) * cv_ref[6][None]
    _, size, cum, row, col = scan_parts(ss_ref[:, maps:], hv_ref[0][None], hv_ref[1][None], span)
    expand = ex_ref[...]
    last = cum[span - 1 : span, :]
    size_e = spread_heads(size, expand)
    ecum_e = spread_heads(jnp.exp(cum), expand)
    tail_e = spread_heads(jnp.exp(last - cum), expand)
    etot_e = spread_heads(jnp.broadcast_to(jnp.exp(last), (8, LANES)), expand)[0:1]
    xs = x * size_e
    xs_low = xs.astype(BF)
    before = state[...]
    before_low = before.astype(BF)
    ent_ref[0] = before_low
    inter = mm(query, before_low) * ecum_e
    state[...] = before * etot_e + t_mm(key, (xs * tail_e).astype(BF))
    inner = mm_t(query, key)
    cum_t = jnp.transpose(cum)
    keepm = row >= col
    left = lax.broadcasted_iota(jnp.int32, (span, LANES), 1) < LANES // 2
    for pair in range(heads // 2):
        lanes = slice(pair * LANES, (pair + 1) * LANES)
        part = []
        for h in (2 * pair, 2 * pair + 1):
            diff = cum[:, h : h + 1] - cum_t[h : h + 1, :]
            mix = jnp.exp(jnp.where(keepm, diff, -1e30)) * inner
            part.append(mm(mix.astype(BF), xs_low[:, lanes]))
        within = jnp.where(left, part[0], part[1])
        ssd_ref[:, lanes] = (within + inter[:, lanes] + x[:, lanes] * cv_ref[5:6, lanes]).astype(ssd_ref.dtype)


def bwd_kernel(
    span, heads, taps_n, vp_ref, vh_ref, ss_ref, sh_ref, dy_ref, ent_ref, cv_ref, cs_ref, hv_ref, ex_ref,
    dv_ref, ds_ref, gcv_ref, gcs_ref, gh_ref, dstate, vbuf, sbuf, dvbuf, dsbuf,
):
    chans = vp_ref.shape[1]
    maps = cs_ref.shape[1]
    nst = maps // 2
    halo = taps_n - 1
    step = pl.program_id(0)
    first = step == 0
    start = step == pl.num_programs(0) - 1

    @pl.when(first)
    def _():
        dstate[...] = jnp.zeros_like(dstate)
        dvbuf[span : span + 8, :] = jnp.zeros((8, chans), F32)
        dsbuf[span : span + 8, :] = jnp.zeros((8, maps), F32)
        gcv_ref[...] = jnp.zeros_like(gcv_ref)
        gcs_ref[...] = jnp.zeros_like(gcs_ref)
        gh_ref[...] = jnp.zeros_like(gh_ref)

    vbuf[0:8, :] = jnp.where(start, 0.0, vh_ref[...].astype(F32))
    sbuf[0:8, :] = jnp.where(start, 0.0, sh_ref[:, :maps])
    vbuf[8 : 8 + span, :] = vp_ref[...].astype(F32)
    sbuf[8 : 8 + span, :] = ss_ref[:, :maps]
    taps = [cv_ref[k] for k in range(taps_n)]
    pre = conv(vbuf, 8 - halo, taps, span) + cv_ref[4][None]
    staps = [cs_ref[k] for k in range(taps_n)]
    spre = conv(sbuf, 8 - halo, staps, span) + cs_ref[4][None]
    ssig = sigmoid(spre)
    sact = spre * ssig
    key = sact[:, :nst].astype(BF)
    query = sact[:, nst:].astype(BF)
    sig = sigmoid(pre)
    keep = cv_ref[6][None]
    x = pre * sig * keep
    rate = hv_ref[1][None]
    raw, size, cum, row, col = scan_parts(ss_ref[:, maps:], hv_ref[0][None], rate, span)
    expand = ex_ref[...]
    last = cum[span - 1 : span, :]
    size_e = spread_heads(size, expand)
    ecum_e = spread_heads(jnp.exp(cum), expand)
    tail_e = spread_heads(jnp.exp(last - cum), expand)
    etot_e = spread_heads(jnp.broadcast_to(jnp.exp(last), (8, LANES)), expand)[0:1]
    xs = x * size_e
    xs_low = xs.astype(BF)
    xt = xs * tail_e
    xt_low = xt.astype(BF)
    dy_low = dy_ref[...].astype(BF)
    dy = dy_low.astype(F32)
    before_low = ent_ref[0]
    dz = dy * ecum_e
    dz_low = dz.astype(BF)
    d_after = dstate[...]
    d_after_low = d_after.astype(BF)
    inter = mm(query, before_low)
    w = mm(key, d_after_low)
    d_query = mm_t(dz_low, before_low)
    d_key = mm_t(xt_low, d_after_low)
    through = jnp.sum(d_after * before_low.astype(F32), axis=0, keepdims=True) * etot_e
    dstate[...] = d_after * etot_e + t_mm(query, dz_low)
    inner_t = mm_t(key, query)
    cum_t = jnp.transpose(cum)
    keepm = row <= col
    lane = lax.broadcasted_iota(jnp.int32, (span, LANES), 1)
    left = lane < LANES // 2
    d_inner_t = jnp.zeros((span, span), F32)
    cols = jnp.zeros((span, LANES), F32)
    rows = []
    dxs_parts = []
    zero = jnp.zeros((span, LANES), BF)
    for pair in range(heads // 2):
        lanes = slice(pair * LANES, (pair + 1) * LANES)
        part = []
        xp = xs_low[:, lanes]
        dyp = dy_low[:, lanes]
        for h, mine in ((2 * pair, left), (2 * pair + 1, jnp.logical_not(left))):
            diff = cum_t[h : h + 1, :] - cum[:, h : h + 1]
            decay = jnp.exp(jnp.where(keepm, diff, -1e30))
            mix = decay * inner_t
            part.append(mm(mix.astype(BF), dyp))
            d_mix = mm_t(jnp.where(mine, xp, zero), dyp) * decay
            d_inner_t = d_inner_t + d_mix
            seg = d_mix * inner_t
            rows.append(jnp.sum(seg, axis=0, keepdims=True))
            cols = cols + jnp.where(lane == h, jnp.sum(seg, axis=1, keepdims=True), 0.0)
        dxs_parts.append(jnp.where(left, part[0], part[1]))
    rows.append(jnp.zeros((LANES - heads, span), F32))
    row_sums = jnp.transpose(jnp.concatenate(rows, axis=0))
    dxs = jnp.concatenate(dxs_parts, axis=1) + w * tail_e
    d_inner_low = d_inner_t.astype(BF)
    d_key = d_key + mm(d_inner_low, query)
    d_query = d_query + t_mm(d_inner_low, key)

    gather = functools.partial(mm_t, b=expand)
    r_inter = gather((dz * inter).astype(BF))
    c_tail = gather((xt * w).astype(BF))
    d_size = gather((dxs * x).astype(BF))
    d_skip = gather((dy * x).astype(BF))
    d_tot = gather(jnp.broadcast_to(through, (8, chans)).astype(BF))[0:1]
    later = (row <= col).astype(BF)
    earlier = (row > col).astype(BF)
    d_la = exact_left(later, row_sums - cols + r_inter) + exact_left(earlier, c_tail) + d_tot
    d_step = (d_size + rate * d_la) * sigmoid(raw)
    gh_ref[0:1, :] = gh_ref[0:1, :] + jnp.sum(d_step, axis=0, keepdims=True)
    gh_ref[1:2, :] = gh_ref[1:2, :] + jnp.sum(d_la * size, axis=0, keepdims=True) * rate
    gh_ref[2:3, :] = gh_ref[2:3, :] + jnp.sum(d_skip, axis=0, keepdims=True)

    d_pre = (dxs * size_e + dy * cv_ref[5][None]) * keep * (sig * (1.0 + pre * (1.0 - sig)))
    dvbuf[0:span, :] = d_pre
    dv = taps[taps_n - 1][None] * d_pre
    for k in range(taps_n - 1):
        dv = dv + taps[k][None] * dvbuf[pl.ds(halo - k, span), :]
    dv_ref[...] = dv.astype(dv_ref.dtype)
    for k in range(taps_n):
        gcv_ref[k : k + 1, :] = gcv_ref[k : k + 1, :] + jnp.sum(
            d_pre * vbuf[pl.ds(8 - halo + k, span), :], axis=0, keepdims=True
        )
    gcv_ref[4:5, :] = gcv_ref[4:5, :] + jnp.sum(d_pre, axis=0, keepdims=True)
    dvbuf[span : span + 8, :] = dvbuf[0:8, :]

    d_spre = jnp.concatenate([d_key, d_query], axis=1) * (ssig * (1.0 + spre * (1.0 - ssig)))
    dsbuf[0:span, :] = d_spre
    dsv = staps[taps_n - 1][None] * d_spre
    for k in range(taps_n - 1):
        dsv = dsv + staps[k][None] * dsbuf[pl.ds(halo - k, span), :]
    ds_ref[:, :maps] = dsv.astype(ds_ref.dtype)
    ds_ref[:, maps:] = d_step.astype(ds_ref.dtype)
    for k in range(taps_n):
        gcs_ref[k : k + 1, :] = gcs_ref[k : k + 1, :] + jnp.sum(
            d_spre * sbuf[pl.ds(8 - halo + k, span), :], axis=0, keepdims=True
        )
    gcs_ref[4:5, :] = gcs_ref[4:5, :] + jnp.sum(d_spre, axis=0, keepdims=True)
    dsbuf[span : span + 8, :] = dsbuf[0:8, :]


def full(shape):
    return pl.BlockSpec(shape, lambda i: (0,) * len(shape))


def scan_fwd(vp, ss, cv, cs, hv, ex, heads, taps_n, span):
    rows, chans = vp.shape
    wide = ss.shape[1]
    maps = cs.shape[1]
    nb = rows // span
    return pl.pallas_call(
        functools.partial(fwd_kernel, span, heads, taps_n),
        grid=(nb,),
        in_specs=[
            pl.BlockSpec((span, chans), lambda i: (i, 0)),
            pl.BlockSpec((span, wide), lambda i: (i, 0)),
            full(cv.shape), full(cs.shape), full(hv.shape), full(ex.shape),
        ],
        out_specs=[
            pl.BlockSpec((span, chans), lambda i: (i, 0)),
            pl.BlockSpec((1, maps // 2, chans), lambda i: (i, 0, 0)),
        ],
        out_shape=[
            jax.ShapeDtypeStruct((rows, chans), F32),
            jax.ShapeDtypeStruct((nb, maps // 2, chans), BF),
        ],
        scratch_shapes=[
            pltpu.VMEM((maps // 2, chans), F32),
            pltpu.VMEM((span + 8, chans), F32),
            pltpu.VMEM((span + 8, maps), F32),
        ],
        compiler_params=pltpu.CompilerParams(
            dimension_semantics=("arbitrary",), vmem_limit_bytes=40 << 20),
        name="scan_fwd",
    )(vp, ss, cv, cs, hv, ex)


def scan_bwd(vp, ss, dy, ent, cv, cs, hv, ex, heads, taps_n, span):
    rows, chans = vp.shape
    wide = ss.shape[1]
    maps = cs.shape[1]
    nb = rows // span
    eights = span // 8
    back = lambda i: (nb - 1 - i, 0)
    halo = lambda i: (jnp.maximum((nb - 1 - i) * eights - 1, 0), 0)
    return pl.pallas_call(
        functools.partial(bwd_kernel, span, heads, taps_n),
        grid=(nb,),
        in_specs=[
            pl.BlockSpec((span, chans), back),
            pl.BlockSpec((8, chans), halo),
            pl.BlockSpec((span, wide), back),
            pl.BlockSpec((8, wide), halo),
            pl.BlockSpec((span, chans), back),
            pl.BlockSpec((1, maps // 2, chans), lambda i: (nb - 1 - i, 0, 0)),
            full(cv.shape), full(cs.shape), full(hv.shape), full(ex.shape),
        ],
        out_specs=[
            pl.BlockSpec((span, chans), back),
            pl.BlockSpec((span, wide), back),
            full((8, chans)), full((8, maps)), full((8, LANES)),
        ],
        out_shape=[
            jax.ShapeDtypeStruct((rows, chans), BF),
            jax.ShapeDtypeStruct((rows, wide), BF),
            jax.ShapeDtypeStruct((8, chans), F32),
            jax.ShapeDtypeStruct((8, maps), F32),
            jax.ShapeDtypeStruct((8, LANES), F32),
        ],
        scratch_shapes=[
            pltpu.VMEM((maps // 2, chans), F32),
            pltpu.VMEM((span + 8, chans), F32),
            pltpu.VMEM((span + 8, maps), F32),
            pltpu.VMEM((span + 8, chans), F32),
            pltpu.VMEM((span + 8, maps), F32),
        ],
        compiler_params=pltpu.CompilerParams(
            dimension_semantics=("arbitrary",), vmem_limit_bytes=48 << 20),
        name="scan_bwd",
    )(vp, vp, ss, ss, dy, ent, cv, cs, hv, ex)


def tables(conv_value, conv_value_bias, conv_state, conv_state_bias, step_bias, decay_log, skip_gain, keep, out_gain):
    heads = step_bias.shape[0]
    chans = conv_value.shape[1]
    head_dim = chans // heads
    row = lambda v: v[None, :]
    wide = lambda v: jnp.repeat(v, head_dim)[None, :]
    cv = jnp.concatenate([conv_value, row(conv_value_bias), wide(skip_gain), wide(keep), row(out_gain)], axis=0)
    cs = jnp.concatenate([conv_state, row(conv_state_bias), jnp.zeros((3, conv_state.shape[1]), F32)], axis=0)
    lanes = lambda v: jnp.pad(v, (0, LANES - heads))[None, :]
    hv = jnp.concatenate([lanes(step_bias), lanes(-jnp.exp(decay_log)), jnp.zeros((6, LANES), F32)], axis=0)
    head_of = lax.broadcasted_iota(jnp.int32, (LANES, chans), 1) // head_dim
    ex = (head_of == lax.broadcasted_iota(jnp.int32, (LANES, chans), 0)).astype(BF)
    return cv, cs, hv, ex


def sums_kernel(ssd_ref, gate_ref, dno_ref, cv_ref, out_ref):
    gate = gate_ref[...].astype(F32)
    gated = ssd_ref[...].astype(F32) * gate * sigmoid(gate)
    squares = jnp.sum(gated * gated, axis=1, keepdims=True)
    stat = jnp.sum(dno_ref[...].astype(F32) * cv_ref[7][None] * gated, axis=1, keepdims=True)
    lane = lax.broadcasted_iota(jnp.int32, (gated.shape[0], LANES), 1)
    both = jnp.where(lane == 0, squares, jnp.where(lane == 1, stat, 0.0))
    out_ref[...] = jnp.transpose(both)[0:8]


def row_sums_of(ssd, gate, dno, cv):
    rows, chans = ssd.shape
    span = 256
    tile = pl.BlockSpec((span, chans), lambda i: (i, 0))
    return pl.pallas_call(
        sums_kernel,
        grid=(rows // span,),
        in_specs=[tile, tile, tile, full(cv.shape)],
        out_specs=pl.BlockSpec((8, span), lambda i: (0, i)),
        out_shape=jax.ShapeDtypeStruct((8, rows), F32),
        compiler_params=pltpu.CompilerParams(
            dimension_semantics=("arbitrary",), vmem_limit_bytes=40 << 20),
        name="row_sums",
    )(ssd, gate, dno, cv)


def norm_kernel(ssd_ref, gate_ref, dno_ref, cv_ref, sums_ref, count_ref, no_ref, dy_ref, dg_ref, og_ref):
    @pl.when(pl.program_id(0) == 0)
    def _():
        og_ref[...] = jnp.zeros_like(og_ref)

    span = ssd_ref.shape[0]
    per = jnp.transpose(jnp.concatenate([sums_ref[...], jnp.zeros((LANES - 8, span), F32)], axis=0))
    count = count_ref[0, 0]
    scale = lax.rsqrt(per[:, 0:1] / count + EPS)
    coef = scale * scale * scale * (per[:, 1:2] / count)
    gate = gate_ref[...].astype(F32)
    ssd = ssd_ref[...].astype(F32)
    sig = sigmoid(gate)
    act = gate * sig
    gated = ssd * act
    gain = cv_ref[7][None]
    dno = dno_ref[...].astype(F32)
    unit = gated * scale
    no_ref[...] = (unit * gain).astype(no_ref.dtype)
    d_gated = dno * gain * scale - gated * coef
    dy_ref[...] = (d_gated * act).astype(dy_ref.dtype)
    dg_ref[...] = (d_gated * ssd * (sig * (1.0 + gate * (1.0 - sig)))).astype(dg_ref.dtype)
    og_ref[0:1, :] = og_ref[0:1, :] + jnp.sum(dno * unit, axis=0, keepdims=True)


def norm_both(ssd, gate, dno, cv, sums, count):
    rows, chans = ssd.shape
    span = 256
    tile = pl.BlockSpec((span, chans), lambda i: (i, 0))
    low = jax.ShapeDtypeStruct((rows, chans), BF)
    return pl.pallas_call(
        norm_kernel,
        grid=(rows // span,),
        in_specs=[
            tile, tile, tile, full(cv.shape),
            pl.BlockSpec((8, span), lambda i: (0, i)),
            pl.BlockSpec(memory_space=pltpu.SMEM),
        ],
        out_specs=[tile, tile, tile, full((8, chans))],
        out_shape=[low, low, low, jax.ShapeDtypeStruct((8, chans), F32)],
        compiler_params=pltpu.CompilerParams(
            dimension_semantics=("arbitrary",), vmem_limit_bytes=40 << 20),
        name="norm_both",
    )(ssd, gate, dno, cv, sums, count)


MESH = pl.DeviceIdType.MESH


def remote(src, dst, sems, at, device):
    return pltpu.make_async_remote_copy(
        src_ref=src, dst_ref=dst, send_sem=sems.at[0, at], recv_sem=sems.at[1, at],
        device_id=device, device_id_type=MESH)


def greet(devices):
    barrier = pltpu.get_barrier_semaphore()
    for device in devices:
        pl.semaphore_signal(barrier, inc=1, device_id=device, device_id_type=MESH)
    pl.semaphore_wait(barrier, len(devices))


def chunks(rows, size, body):
    def step(i, carry):
        body(pl.ds(pl.multiple_of(i * size, size), size))
        return carry

    lax.fori_loop(0, rows // size, step, 0)


class RingSum:
    def __init__(self, parts, slots, sems, dp, head):
        self.parts, self.slots, self.sems = parts, slots, sems
        z, x = dp // 2, lax.rem(dp, 2)
        self.place = z * (1 - x) + (7 - z) * x
        self.head = head
        self.half = slots.shape[2]
        self.sent = []

    def block(self, shift):
        at = lax.rem(self.place + shift + 16, 8)
        x = at // 4
        return (at * (1 - x) + (7 - at) * x) * 2 + x

    def send(self, hop):
        for way in range(2):
            sign = 1 - 2 * way
            if hop == 0:
                source = self.parts.at[self.block(-sign), pl.ds(way * self.half, self.half)]
            else:
                source = self.slots.at[way, hop - 1]
            copy = pltpu.make_async_remote_copy(
                src_ref=source, dst_ref=self.slots.at[way, hop],
                send_sem=self.sems.at[0, way, hop], recv_sem=self.sems.at[1, way, hop],
                device_id=(self.block(sign), self.head), device_id_type=MESH)
            copy.start()
            self.sent.append(copy)

    def start(self):
        self.send(0)

    def step(self, hop):
        for way in range(2):
            self.sent[2 * hop + way].wait_recv()
            block = self.block((2 * way - 1) * (2 + hop))

            def add(rows):
                low = pl.ds(pl.multiple_of(rows.start + way * self.half, 32), 32)
                self.slots[way, hop, rows, :] = (
                    self.slots[way, hop, rows, :].astype(F32) + self.parts[block, low, :].astype(F32)).astype(BF)

            chunks(self.half, 32, add)
        self.send(hop + 1)

    def finish(self, emit):
        mine = self.block(0)
        for way in range(2):
            self.sent[12 + way].wait_recv()

            def add(rows):
                low = pl.ds(pl.multiple_of(rows.start + way * self.half, 32), 32)
                emit(low, self.slots[way, 6, rows, :].astype(F32) + self.parts[mine, low, :].astype(F32))

            chunks(self.half, 32, add)
        for copy in self.sent:
            copy.wait_send()


class OverHead:
    def __init__(self, source, local, got, total, got2, sems, copy_sem, place):
        self.source, self.local, self.got, self.total, self.got2, self.sems = source, local, got, total, got2, sems
        self.y, self.core, self.over_core, self.over_y = place
        self.keep = pltpu.make_async_copy(source.at[:, self.core], local, copy_sem)

    def start(self):
        self.copies = []
        for i in range(2):
            row = lax.rem(self.y + 1 + i, 2)
            copy = remote(self.source.at[row, 1 - self.core], self.got.at[i], self.sems, i, self.over_core)
            copy.start()
            self.copies.append(copy)
        self.keep.start()

    def middle(self):
        self.keep.wait()
        self.copies[0].wait_recv()
        rows_n = self.got2.shape[0]
        parts = 4
        size = rows_n // parts
        self.cross = []
        for part in range(parts):
            def add(rows):
                at = pl.ds(pl.multiple_of(part * size + rows.start, 16), 16)
                self.total[at, :] = (
                    self.local[1 - self.y, at, :].astype(F32) + self.got[0, at, :].astype(F32)).astype(BF)

            chunks(size, 16, add)
            at = pl.ds(part * size, size)
            copy = remote(self.total.at[at], self.got2.at[at], self.sems, 2 + part, self.over_y)
            copy.start()
            self.cross.append(copy)

    def finish(self, emit):
        self.copies[1].wait_recv()
        for copy in self.cross:
            copy.wait_recv()

        def add(rows):
            emit(rows, self.local[self.y, rows, :].astype(F32) + self.got[1, rows, :].astype(F32)
                 + self.got2[rows, :].astype(F32))

        chunks(self.got2.shape[0], 16, add)
        for copy in (*self.copies, *self.cross):
            copy.wait_send()


def places():
    dp, head = lax.axis_index("dp"), lax.axis_index("head")
    y, core = head // 2, lax.rem(head, 2)
    over_core = (dp, y * 2 + 1 - core)
    over_y = (dp, (1 - y) * 2 + core)
    return dp, head, (y, core, over_core, over_y)


def closing_kernel(
    model, maps,
    go_ref, gg_ref, gv_ref, gs_ref, op_ref, dn_ref, hid_ref, cot_ref, gain_ref, gcv_ref, og_ref, gh_ref, gcs_ref,
    block_ref, ingrad_ref, og_out, gg_out, gv_out, gs_out, small1, small2,
    *scratch,
):
    (slots_o, sems_o, slots_g, sems_g, slots_v, sems_v, slots_s, sems_d) = scratch[:8]
    heads_set = [scratch[8 + 4 * i : 12 + 4 * i] for i in range(2)]
    (copy_sems, sems_h0, sems_h1, small_in1, small_in2, got_s2, got_s1b, got_s2b, state_own, got_state,
     sems_s, ig_acc) = scratch[16:]
    dp, head, head_place = places()
    peers_head = [(dp, lax.rem(head + k, 4)) for k in range(1, 4)]
    peers_dp = [(lax.rem(dp + k, 8), head) for k in range(1, 8)]
    greet(peers_head + peers_dp)

    out_w = RingSum(go_ref, slots_o, sems_o, dp, head)
    gate_w = RingSum(gg_ref, slots_g, sems_g, dp, head)
    value_w = RingSum(gv_ref, slots_v, sems_v, dp, head)
    side_w = RingSum(gs_ref, slots_s, sems_d, dp, head)
    d_normed = OverHead(dn_ref, *heads_set[0], sems_h0, copy_sems.at[0], head_place)
    own_out = OverHead(op_ref, *heads_set[1], sems_h1, copy_sems.at[1], head_place)
    d_normed.start()
    side_w.start()
    out_w.start()
    gate_w.start()
    value_w.start()
    own_out.start()
    d_normed.middle()
    for hop in range(6):
        side_w.step(hop)
        out_w.step(hop)
        if hop == 0:
            own_out.middle()
        gate_w.step(hop)
        value_w.step(hop)

    def give_state(rows, value):
        gs_out[rows, :] = value

    side_w.finish(give_state)
    state_own[...] = gs_out[:, :maps].astype(BF)
    state_copies = []
    for k, peer in enumerate(peers_head):
        copy = remote(state_own, got_state.at[k], sems_s, k, peer)
        copy.start()
        state_copies.append(copy)

    ig_acc[...] = jnp.zeros_like(ig_acc)

    def give_in(rows, d_n):
        resid = hid_ref[rows, :].astype(F32)
        scale = lax.rsqrt(jnp.mean(resid * resid, axis=-1, keepdims=True) + EPS)
        scaled = d_n * gain_ref[...]
        ingrad_ref[rows, :] = (
            cot_ref[rows, :].astype(F32) + scaled * scale
            - resid * (scale * scale * scale * (jnp.sum(scaled * resid, axis=-1, keepdims=True) / model)))
        ig_acc[0:1, :] = ig_acc[0:1, :] + jnp.sum(d_n * resid * scale, axis=0, keepdims=True)

    d_normed.finish(give_in)
    wide = small_in2.shape[1]
    small_in2[...] = jnp.zeros_like(small_in2)
    for i in range(model // wide):
        small_in2[i : i + 1, :] = ig_acc[0:1, i * wide : (i + 1) * wide]
    per = wide // maps
    for k in range(5):
        row = model // wide + k // per
        lanes = slice((k % per) * maps, (k % per + 1) * maps)
        small_in2[row : row + 1, lanes] = gcs_ref[k : k + 1, :]
    small_in1[...] = gcv_ref[...]
    small_in1[5:6, :] = og_ref[0:1, :]
    for k in range(3):
        small_in1[6:7, k * LANES : (k + 1) * LANES] = gh_ref[k : k + 1, :]
    first = []
    for k, peer in enumerate(peers_head):
        copy = remote(small_in2, got_s2.at[k], sems_s, 3 + k, peer)
        copy.start()
        first.append(copy)
    second = []
    for k, peer in enumerate(peers_dp):
        copy = remote(small_in1, got_s1b.at[k], sems_s, 6 + k, peer)
        copy.start()
        second.append(copy)
    for copy in first:
        copy.wait_recv()
    small2[...] = small_in2[...] + got_s2[0] + got_s2[1] + got_s2[2]
    third = []
    for k, peer in enumerate(peers_dp):
        copy = remote(small2, got_s2b.at[k], sems_s, 13 + k, peer)
        copy.start()
        third.append(copy)

    def give_out(rows, value):
        block_ref[rows, :] = (hid_ref[rows, :].astype(F32) + value).astype(BF)

    own_out.finish(give_out)

    def give(ref):
        def emit(rows, value):
            ref[rows, :] = value
        return emit

    out_w.finish(give(og_out))
    gate_w.finish(give(gg_out))
    for copy in state_copies:
        copy.wait_recv()
    gs_out[:, :maps] = gs_out[:, :maps] + got_state[0].astype(F32) + got_state[1].astype(F32) + got_state[2].astype(F32)
    value_w.finish(give(gv_out))
    for copy in (*second, *third):
        copy.wait_recv()
    for copy in third:
        copy.wait_send()
    total1, total2 = small_in1[...], small2[...]
    for k in range(7):
        total1 = total1 + got_s1b[k]
        total2 = total2 + got_s2b[k]
    small1[...] = total1
    small2[...] = total2
    for copy in (*first, *second, *state_copies):
        copy.wait_send()


def closing(go, gg, gv, gs, op, dn, hidden, cot, in_gain, gcv, og, gh, gcs):
    model = hidden.shape[1]
    maps = gcs.shape[1]
    rows = hidden.shape[0]
    block = go.shape[1:]
    side = gs.shape[1:]
    anyspace = pl.BlockSpec(memory_space=pl.ANY)
    vmem = pl.BlockSpec(memory_space=pltpu.VMEM)
    sem = pltpu.SemaphoreType.DMA

    def head_set():
        return [
            pltpu.VMEM((2, rows, model), BF), pltpu.VMEM((2, rows, model), BF),
            pltpu.VMEM((rows, model), BF), pltpu.VMEM((rows, model), BF),
        ]

    scratch = []
    for shape in (block, block, block, side):
        scratch += [pltpu.VMEM((2, 7, shape[0] // 2, shape[1]), BF), sem((2, 2, 7))]
    for _ in range(2):
        scratch += head_set()
    small = pltpu.VMEM((8, 1024), F32)
    extra = [
        sem((2,)), sem((2, 6)), sem((2, 6)), small, small,
        pltpu.VMEM((3, 8, 1024), F32), pltpu.VMEM((7, 8, 1024), F32), pltpu.VMEM((7, 8, 1024), F32),
        pltpu.VMEM((rows, maps), BF), pltpu.VMEM((3, rows, maps), BF), sem((2, 20)),
        pltpu.VMEM((8, model), F32),
    ]
    return pl.pallas_call(
        functools.partial(closing_kernel, model, maps),
        in_specs=[vmem] * 4 + [anyspace] * 2 + [vmem] * 7,
        out_specs=[vmem] * 8,
        out_shape=[
            jax.ShapeDtypeStruct((rows, model), BF), jax.ShapeDtypeStruct((rows, model), F32),
            jax.ShapeDtypeStruct(block, F32), jax.ShapeDtypeStruct(block, F32),
            jax.ShapeDtypeStruct(block, F32), jax.ShapeDtypeStruct(side, F32),
            jax.ShapeDtypeStruct((8, 1024), F32), jax.ShapeDtypeStruct((8, 1024), F32),
        ],
        scratch_shapes=scratch + extra,
        compiler_params=pltpu.CompilerParams(
            collective_id=0, has_side_effects=True, vmem_limit_bytes=60 << 20),
        name="closing",
    )(go, gg, gv, gs, op, dn, hidden, cot, in_gain[None, :], gcv, og, gh, gcs)


def per_device(
    hidden_in, in_gain, gate_proj, value_proj, state_proj, step_proj, conv_value, conv_value_bias,
    conv_state, conv_state_bias, step_bias, decay_log, skip_gain, out_gain, out_proj, cotangent, width_level,
):
    heads = step_bias.shape[0]
    chans = conv_value.shape[1]
    head_dim = chans // heads
    maps = conv_state.shape[1]
    taps_n = conv_value.shape[0]
    groups = lax.axis_size("head")
    model = hidden_in.shape[1]
    assert width_level.shape[0] == 1 and 2 * head_dim == LANES and heads <= LANES
    span = 128

    resid = hidden_in.astype(F32)
    in_scale = lax.rsqrt(jnp.mean(resid * resid, axis=-1, keepdims=True) + EPS)
    normed = (resid * in_scale * in_gain).astype(BF)
    whole = lax.all_gather(normed, "head", axis=0, tiled=True)
    cot_all = lax.all_gather(cotangent, "head", axis=0, tiled=True)
    side_proj = jnp.concatenate(
        [state_proj, step_proj, jnp.zeros((model, LANES - heads), BF)], axis=1)

    active = jnp.right_shift(heads, 3 - width_level[0])
    keep = (jnp.arange(heads) < active).astype(F32)
    count = (active * groups * head_dim).astype(F32).reshape(1, 1)
    cv, cs, hv, ex = tables(
        conv_value, conv_value_bias, conv_state, conv_state_bias, step_bias, decay_log, skip_gain, keep, out_gain)

    value_pre = mm(whole, value_proj)
    side_pre = mm(whole, side_proj)
    gate_pre = mm(whole, gate_proj)
    ssd, entering = scan_fwd(value_pre, side_pre, cv, cs, hv, ex, heads, taps_n, span)
    d_normed_out = mm_t(cot_all, out_proj)
    sums = row_sums_of(ssd, gate_pre, d_normed_out, cv)
    sums = jnp.pad(lax.psum(sums[:2], "head"), ((0, 6), (0, 0)))
    normed_out, dy, d_gate, og = norm_both(ssd, gate_pre, d_normed_out, cv, sums, count)
    out_part = mm(normed_out, out_proj).astype(BF)
    part_out = t_mm(cot_all, normed_out).astype(BF)
    part_gate = t_mm(whole, d_gate).astype(BF)
    d_value, d_side, gcv, gcs, gh = scan_bwd(
        value_pre, side_pre, dy, entering, cv, cs, hv, ex, heads, taps_n, span)
    part_value = t_mm(whole, d_value).astype(BF)
    d_normed = (mm_t(d_gate, gate_proj) + mm_t(d_value, value_proj) + mm_t(d_side, side_proj)).astype(BF)
    part_side = t_mm(whole, d_side).astype(BF)
    if lax.axis_size("dp") == 8 and groups == 4 and chans == 1024 and model == 2 * chans:
        by_dp = lambda v: v.reshape(8, model // 8, v.shape[1])
        by_head = lambda v: v.reshape(2, 2, v.shape[0] // 4, model)
        (block_out, in_grad, out_proj_grad, gate_proj_grad, value_proj_grad, side_grad, small1, small2) = closing(
            by_dp(part_out), by_dp(part_gate), by_dp(part_value), by_dp(part_side), by_head(out_part),
            by_head(d_normed), hidden_in, cotangent, in_gain, gcv, og, gh, gcs)
        out_proj_grad = out_proj_grad.T
        state_proj_grad = side_grad[:, :maps]
        step_proj_grad = side_grad[:, maps : maps + heads]
        gcv, og = small1, small1[5]
        gh = jnp.pad(small1[6, : 3 * LANES].reshape(3, LANES), ((0, 5), (0, 0)))
        in_gain_grad = small2[: model // chans].reshape(model)
        gcs = small2[model // chans : model // chans + 2].reshape(-1, maps)
    else:
        over_dp = lambda v: lax.psum_scatter(v, "dp", scatter_dimension=0, tiled=True).astype(F32)
        over_head = lambda v: lax.psum_scatter(v, "head", scatter_dimension=0, tiled=True).astype(F32)
        block_out = (resid + over_head(out_part)).astype(BF)
        d_normed = over_head(d_normed)
        scaled = d_normed * in_gain
        in_grad = (
            cotangent.astype(F32) + scaled * in_scale
            - resid * in_scale**3 * jnp.sum(scaled * resid, axis=-1, keepdims=True) / model
        )
        out_proj_grad = over_dp(part_out).T
        gate_proj_grad, value_proj_grad, side_grad = over_dp(part_gate), over_dp(part_value), over_dp(part_side)
        step_proj_grad = side_grad[:, maps : maps + heads]
        in_gain_grad, gcs, state_proj_grad = lax.psum(
            (jnp.sum(d_normed * resid * in_scale, axis=0), gcs, side_grad[:, :maps]), "head")
        in_gain_grad, gcs, gcv, gh, og = lax.psum((in_gain_grad, gcs, gcv, gh, og[0]), "dp")
    return (
        block_out, in_grad, in_gain_grad, gate_proj_grad, value_proj_grad, state_proj_grad, step_proj_grad,
        gcv[:taps_n], gcv[4], gcs[:taps_n], gcs[4], gh[0, :heads], gh[1, :heads], gh[2, :heads], og, out_proj_grad,
    )


def solution(mesh):
    placed = (
        P(("dp", "head"), None),
        P(),
        P(None, "head"),
        P(None, "head"),
        P(),
        P(None, "head"),
        P(None, "head"),
        P("head"),
        P(),
        P(),
        P("head"),
        P("head"),
        P("head"),
        P("head"),
        P("head", None),
        P(("dp", "head"), None),
        P("dp"),
    )
    return jax.shard_map(
        per_device,
        mesh=mesh,
        in_specs=placed,
        out_specs=(
            P(("dp", "head"), None),
            P(("dp", "head"), None),
            P(),
            P("dp", "head"),
            P("dp", "head"),
            P("dp", None),
            P("dp", "head"),
            P(None, "head"),
            P("head"),
            P(),
            P(),
            P("head"),
            P("head"),
            P("head"),
            P("head"),
            P("head", "dp"),
        ),
        check_vma=False,
    )
```
